32 devices in a mesh: grp: 2 (over y), gy: 4 (over z), gx: 2 (over x), ch: 2 (over core).
Axes of the slice: x: 2, y: 2, z: 4, core: 2. Of those that a mesh axis runs over, the one named last changes fastest.
Arguments:
- cells: bfloat16 [128, 128, 512], P(('grp', 'gy'), 'gx'), parts along dimension 0, may hold values from -6 to 6
- w_expand: bfloat16 [512, 2048], P(None, 'ch'), may hold values from -0.25 to 0.25
- b_expand: float32 [2048], P('ch'), may hold values from -3 to 3
- w_depth: bfloat16 [3, 3, 2048], P(None, None, 'ch'), may hold values from -2 to 2
- b_depth: float32 [2048], P('ch'), may hold values from -3 to 3
- w_project: bfloat16 [2048, 512], P('ch'), may hold values from -0.125 to 0.125
- b_project: float32 [512], replicated, may hold values from -3 to 3
- ln_gain: float32 [512], replicated, may hold values from 0.5 to 1.5
- w_qkv: bfloat16 [512, 3, 512], P(None, None, 'ch'), as said below
- w_out: bfloat16 [512, 512], P('ch'), may hold values from -0.25 to 0.25
- b_out: float32 [512], P('ch'), may hold values from -3 to 3
Outputs:
- result: bfloat16 [128, 128, 512], P(('grp', 'gy'), 'gx', 'ch'), parts along dimension 0
The draws below stay inside these ranges and needn't reach their ends.
There are 2 independent parts, one for each index of `grp`. The reference program is written for one: setup_inputs(seed, part) draws one part's arguments, and reference() takes and returns one part's arrays. A program takes and returns all parts, laid end to end along the dimension named above; an argument that names none is the same for every part. Nothing has to cross between parts.
Inputs may be any that keep to these rules, and one draw needn't show every extreme that they name: `w_qkv`: dense projection weights of every head.
All inputs are finite; a program needn't handle non-finite values.
Results may differ from the reference program's by a relative error of at most 0.01.
Values may be sent and summed in bfloat16 or wider, within the bound.
A program may use at most 64 MiB of HBM per device.

```python
import jax
import jax.numpy as jnp
from jax import lax

C = 512
EXP = 2048
HEADS = 16
HEAD_DIM = 32
GRID = 8
ROWS = 64
COLS = 128


def draw_w_qkv(key, part):
    key_base = jax.random.fold_in(key, 11)
    weight_scale = C ** (-0.5)
    return (jax.random.normal(key_base, (C, 3, C), jnp.float32) * weight_scale).astype(jnp.bfloat16)


def levels(own_key, dims, pieces, least, high):
    gain = 1.0
    for position, blocks in pieces:
        draws = jax.random.uniform(jax.random.fold_in(jax.random.fold_in(own_key, 6), position), (blocks,), jnp.float32, least / len(pieces), high / len(pieces))
        gain = gain * jnp.repeat(jnp.exp(draws), dims[position] // blocks).reshape((-1,) + (1,) * (len(dims) - 1 - position))
    return gain


def normal_values(stream_key, extent, scale, bound, split=(), kind=jnp.bfloat16):
    gain = levels(stream_key, extent, split, -0.22, 0.18) if split else 1.0
    values = jax.random.normal(stream_key, extent, jnp.float32) * scale * gain
    return jnp.minimum(jnp.maximum(values, -bound), bound).astype(kind)


def setup_inputs(seed: int = 0, part: int = 0) -> dict:
    splits = jax.random.split(jax.random.key(seed), 12)
    part_splits = jax.random.split(jax.random.fold_in(splits[11], part), 12)
    return {
        "cells": normal_values(part_splits[0], (ROWS, COLS, C), 1.0, 6.0, ((0, 4), (1, 2))),
        "w_expand": normal_values(splits[1], (C, EXP), C ** -0.5, 0.25, ((1, 2),)),
        "b_expand": normal_values(splits[2], (EXP,), 0.5, 3.0, ((0, 2),), jnp.float32),
        "w_depth": normal_values(splits[3], (3, 3, EXP), 9 ** -0.5, 2.0, ((2, 2),)),
        "b_depth": normal_values(splits[4], (EXP,), 0.5, 3.0, ((0, 2),), jnp.float32),
        "w_project": normal_values(splits[5], (EXP, C), EXP ** -0.5, 0.125, ((0, 2),)),
        "b_project": normal_values(splits[6], (C,), 0.5, 3.0, (), jnp.float32),
        "ln_gain": jnp.clip(jax.random.uniform(splits[7], (C,), jnp.float32, 0.5, 1.5), 0.5, 1.5),
        "w_qkv": draw_w_qkv(jax.random.fold_in(splits[11], 71), part),
        "w_out": normal_values(splits[9], (C, C), C ** -0.5, 0.25, ((0, 2),)),
        "b_out": normal_values(splits[10], (C,), 0.5, 3.0, ((0, 2),), jnp.float32),
    }


def gelu_exact(values):
    return jax.nn.gelu(values, approximate=False)

def normalize(source, ln_gain):
    values = source.astype(jnp.float32)
    centre = lax.optimization_barrier(jnp.mean(values, axis=-1, keepdims=True))
    centered = values - centre
    spread = lax.optimization_barrier(jnp.mean(centered * centered, axis=-1, keepdims=True))
    return (centered * lax.rsqrt(spread + 1e-05) * ln_gain).astype(jnp.bfloat16)

def reference(cells, w_expand, b_expand, w_depth, b_depth, w_project, b_project, ln_gain, w_qkv, w_out, b_out):
    rows, cols, width = cells.shape
    blocks = 8
    piece = EXP // blocks
    expand_blocks = w_expand.reshape(width, blocks, piece).transpose(1, 0, 2)
    bias_blocks = b_expand.reshape(blocks, piece)
    depth_blocks = w_depth.reshape(3, 3, blocks, piece).transpose(2, 0, 1, 3)
    depth_bias = b_depth.reshape(blocks, piece)
    project_blocks = w_project.reshape(blocks, piece, width)
    flat_cells = cells.reshape(rows * cols, width)

    def add_block(total, parts):
        w_e, b_e, w_d, b_d, w_p = parts
        pre = jnp.dot(flat_cells, w_e, preferred_element_type=jnp.float32).reshape(rows, cols, piece)
        expanded = gelu_exact(pre + b_e).astype(jnp.bfloat16)
        padded = jnp.pad(expanded, ((1, 1), (1, 1), (0, 0)))
        summed = jnp.zeros((rows, cols, piece), jnp.float32)
        for row_off in range(3):
            for col_off in range(3):
                summed = summed + padded[row_off:row_off + rows, col_off:col_off + cols].astype(jnp.float32) * w_d[row_off, col_off].astype(jnp.float32)
        depth = gelu_exact(summed + b_d).astype(jnp.bfloat16)
        term = jnp.dot(depth.reshape(rows * cols, piece), w_p, preferred_element_type=jnp.float32)
        return (total + term.reshape(rows, cols, width), None)
    total, _ = lax.scan(add_block, jnp.zeros((rows, cols, width), jnp.float32), (expand_blocks, bias_blocks, depth_blocks, depth_bias, project_blocks))
    mixed = (cells.astype(jnp.float32) + total + b_project).astype(jnp.bfloat16)
    stride_h = rows // GRID
    stride_w = cols // GRID
    windows = mixed.reshape(GRID, stride_h, GRID, stride_w, width).transpose(1, 3, 0, 2, 4)
    windows = windows.reshape(stride_h * stride_w, GRID * GRID, width)
    count = stride_h * stride_w
    tokens = GRID * GRID
    normed = normalize(windows, ln_gain).reshape(count * tokens, width)

    def project_heads(index):
        projected = jnp.dot(normed, w_qkv[:, index, :], preferred_element_type=jnp.float32).astype(jnp.bfloat16)
        return projected.reshape(count, tokens, HEADS, HEAD_DIM).transpose(2, 0, 1, 3)
    query = project_heads(0)
    keyset = project_heads(1)
    valueset = project_heads(2)

    def one_head(parts):
        head_q, head_k, head_v = parts
        scores = jnp.einsum('wqd,wkd->wqk', head_q.astype(jnp.float32), head_k.astype(jnp.float32)) * HEAD_DIM ** (-0.5)
        weights = jax.nn.softmax(scores, axis=-1).astype(jnp.bfloat16)
        return jnp.einsum('wqk,wkd->wqd', weights.astype(jnp.float32), head_v.astype(jnp.float32)).astype(jnp.bfloat16)
    heads_out = lax.map(one_head, (query, keyset, valueset))
    attended = heads_out.transpose(1, 2, 0, 3).reshape(count * tokens, width)
    projected_out = jnp.dot(attended, w_out, preferred_element_type=jnp.float32).reshape(count, tokens, width)
    outcome = (windows.astype(jnp.float32) + projected_out + b_out).astype(jnp.bfloat16)
    outcome = outcome.reshape(stride_h, stride_w, GRID, GRID, width).transpose(2, 0, 3, 1, 4)
    return outcome.reshape(rows, cols, width)
```

```python
import functools

import jax
import jax.numpy as jnp
import numpy as np
from jax import lax
from jax.experimental import pallas as pl
from jax.experimental.pallas import tpu as pltpu
from jax.sharding import PartitionSpec as P

HEAD_DIM = 32
GRID = 8
MESH = pl.DeviceIdType.MESH
F32 = jnp.float32
BF16 = jnp.bfloat16


def gelu(v):
    return v * (0.5 * (1.0 + lax.erf(v * np.float32(np.sqrt(0.5)))))


def dot(a, b):
    return jnp.dot(a, b, preferred_element_type=F32)


class Plan:
    def __init__(self, mesh_shape, tile_h, tile_w):
        self.n_rows, self.n_cols = mesh_shape["gy"], mesh_shape["gx"]
        self.tile_h, self.tile_w = tile_h, tile_w
        stride_h = tile_h * self.n_rows // GRID
        stride_w = tile_w * self.n_cols // GRID
        self.depth_h, self.depth_w = min(tile_h, stride_h), min(tile_w, stride_w)
        self.steps_h, self.steps_w = stride_h // self.depth_h, stride_w // self.depth_w
        self.n_i, self.n_j = tile_h // self.depth_h, tile_w // self.depth_w
        self.ph, self.pw = GRID // self.n_i, GRID // self.n_j
        self.own_h, self.own_w = self.depth_h // self.ph, self.depth_w // self.pw
        assert self.own_h == 2
        self.n_t = self.n_i * self.n_j
        self.sources = self.ph * self.pw
        self.piece = self.own_w * self.n_t
        self.slab = self.n_i * tile_w
        groups = self.own_w
        while groups > 1 and (self.piece // groups) % 16:
            groups //= 2
        self.groups = groups
        self.span = self.piece // groups

    def permutation(self):
        out = np.zeros((self.slab, self.slab), np.float32)
        for q in range(self.pw):
            for b in range(self.own_w):
                for i in range(self.n_i):
                    for j in range(self.n_j):
                        row = (q * self.own_w + b) * self.n_t + i * self.n_j + j
                        out[row, i * self.tile_w + j * self.depth_w + q * self.own_w + b] = 1
        return out

    def score_bias(self):
        rows = np.arange(self.sources * self.span)
        window = (rows % self.span) // self.n_t
        return np.where(window[:, None] == window[None, :], 0.0, -1e30).astype(np.float32)


def kernel(
    plan, cells, w_exp, b_exp, w_dep, b_dep, w_proj, b_proj, gain, w_qkv, w_out, b_out,
    perm, perm_t, bias_s, edge_own, out,
    exp, halo, edge, colin, colexp, dbuf, psend, precv, acc, fsend, frecv,
    wq_other, wo_other, bo_full, osend, oin,
    halo_s, halo_r, col_s, col_r, w_s, w_r, p_s, p_r, f_s, f_r, o_s, o_r,
):
    tile_h, tile_w = plan.tile_h, plan.tile_w
    width = cells.shape[2]
    inner = w_exp.shape[1]
    half = width // 2
    z, x, c = lax.axis_index("gy"), lax.axis_index("gx"), lax.axis_index("ch")
    zs, xs = lax.rem(z, plan.steps_h), lax.rem(x, plan.steps_w)
    mp, mq = lax.div(z, plan.steps_h), lax.div(x, plan.steps_w)
    my_s = mp * plan.pw + mq
    last_z, last_x = plan.n_rows - 1, plan.n_cols - 1
    partner = {"ch": 1 - c}
    has_top, has_bot = z > 0, z < last_z
    has_left, has_right = x > 0, x < last_x

    def peer(s, core):
        p, q = lax.div(s, plan.pw), lax.rem(s, plan.pw)
        return {"gy": p * plan.steps_h + zs, "gx": q * plan.steps_w + xs, "ch": core}

    def remote(src, dst, send, recv, device):
        return pltpu.make_async_remote_copy(
            src_ref=src, dst_ref=dst, send_sem=send, recv_sem=recv,
            device_id=device, device_id_type=MESH,
        )

    barrier = pltpu.get_barrier_semaphore()
    around = (
        (has_top, {"gy": jnp.maximum(z - 1, 0)}),
        (has_bot, {"gy": jnp.minimum(z + 1, last_z)}),
        (has_left, {"gx": jnp.maximum(x - 1, 0)}),
        (has_right, {"gx": jnp.minimum(x + 1, last_x)}),
    )
    count = jnp.int32(2 * plan.sources - 1)
    for there, device in around:
        @pl.when(there)
        def _():
            pl.semaphore_signal(barrier, inc=1, device_id=device, device_id_type=MESH)
        count = count + there.astype(jnp.int32)

    @pl.loop(0, 2 * plan.sources)
    def _(t):
        s, core = lax.div(t, 2), lax.rem(t, 2)

        @pl.when(jnp.logical_not((s == my_s) & (core == c)))
        def _():
            pl.semaphore_signal(barrier, inc=1, device_id=peer(s, core), device_id_type=MESH)

    pl.semaphore_wait(barrier, count)

    down = remote(cells.at[tile_h - 1], halo.at[0], halo_s.at[0], halo_r.at[0], around[1][1])
    up = remote(cells.at[0], halo.at[1], halo_s.at[1], halo_r.at[1], around[0][1])
    rightward = remote(edge.at[1], colin.at[0], col_s.at[0], col_r.at[0], around[3][1])
    leftward = remote(edge.at[0], colin.at[1], col_s.at[1], col_r.at[1], around[2][1])
    weights = (
        remote(w_qkv, wq_other, w_s.at[0], w_r.at[0], partner),
        remote(w_out, wo_other, w_s.at[1], w_r.at[1], partner),
        remote(b_out, bo_full.at[c], w_s.at[2], w_r.at[2], partner),
    )

    @pl.when(has_bot)
    def _():
        down.start()

    @pl.when(has_top)
    def _():
        up.start()

    for copy in weights:
        copy.start()
    bo_full[c] = b_out[...]

    lanes_e = 256
    rows_e = 4

    def expand(source, lanes):
        return gelu(dot(source, w_exp[:, lanes]) + b_exp[:, lanes])

    def expand_rows(first):
        source = cells[pl.ds(first, rows_e)].reshape(rows_e * tile_w, width)

        @pl.loop(0, inner // lanes_e)
        def _(t):
            lanes = pl.ds(pl.multiple_of(t * lanes_e, lanes_e), lanes_e)
            value = expand(source, lanes)
            for r in range(rows_e):
                exp[first + 1 + r, 0:tile_w, lanes] = value[r * tile_w : (r + 1) * tile_w]

    @pl.loop(0, tile_h // rows_e // 2)
    def _(t):
        expand_rows(t * rows_e)

    for index, there, copy in ((0, has_top, down), (1, has_bot, up)):
        @pl.when(there)
        def _():
            copy.wait_recv()

        @pl.when(jnp.logical_not(there))
        def _():
            halo[index] = jnp.zeros(halo.shape[1:], BF16)

    flat = cells[...].reshape(tile_h * tile_w, width)
    span_rows = edge.shape[1]
    picked = dot(edge_own[...], flat)
    at_row = lax.broadcasted_iota(jnp.int32, (span_rows, width), 0)
    for side, col in ((0, 0), (1, tile_w - 1)):
        top = halo[0].astype(F32)[col : col + 1]
        bottom = halo[1].astype(F32)[col : col + 1]
        value = picked[side * span_rows : (side + 1) * span_rows]
        value = jnp.where(at_row == 0, top, jnp.where(at_row == tile_h + 1, bottom, value))
        edge[side] = value.astype(BF16)

    @pl.when(has_right)
    def _():
        rightward.start()

    @pl.when(has_left)
    def _():
        leftward.start()

    @pl.loop(tile_h // rows_e // 2, tile_h // rows_e)
    def _(t):
        expand_rows(t * rows_e)

    ok_top, ok_bot = has_top.astype(F32), has_bot.astype(F32)
    ok_left, ok_right = has_left.astype(F32), has_right.astype(F32)
    halo_flat = halo[...].reshape(2 * tile_w, width)

    @pl.loop(0, inner // lanes_e)
    def _(t):
        lanes = pl.ds(pl.multiple_of(t * lanes_e, lanes_e), lanes_e)
        value = expand(halo_flat, lanes)
        exp[0, 0:tile_w, lanes] = value[:tile_w] * ok_top
        exp[tile_h + 1, 0:tile_w, lanes] = value[tile_w:] * ok_bot

    for index, there, copy in ((0, has_left, rightward), (1, has_right, leftward)):
        @pl.when(there)
        def _():
            copy.wait_recv()

        @pl.when(jnp.logical_not(there))
        def _():
            colin[index] = jnp.zeros(colin.shape[1:], BF16)

    col_flat = colin[...].reshape(2 * span_rows, width)

    @pl.loop(0, inner // lanes_e)
    def _(t):
        lanes = pl.ds(pl.multiple_of(t * lanes_e, lanes_e), lanes_e)
        colexp[:, lanes] = expand(col_flat, lanes)

    @pl.loop(0, tile_h + 2)
    def _(r):
        row_ok = jnp.where(r == 0, ok_top, jnp.where(r == tile_h + 1, ok_bot, jnp.float32(1)))
        left = colexp[pl.ds(r, 1), :] * (row_ok * ok_left)
        right = colexp[pl.ds(span_rows + r, 1), :] * (row_ok * ok_right)
        at = lax.broadcasted_iota(jnp.int32, (8, inner), 0)
        exp[r, tile_w : tile_w + 8, :] = jnp.where(at == 0, right, left)

    lanes_d = 128
    wide = tile_w + 8

    def partial_copy(p):
        return remote(psend.at[p], precv.at[p], p_s.at[p], p_r.at[p], partner)

    def depth_rows(p):
        @pl.loop(0, 2 * plan.n_i * (inner // lanes_d))
        def _(t):
            chunk = lax.rem(t, inner // lanes_d)
            which = lax.div(t, inner // lanes_d)
            i, kk = lax.rem(which, plan.n_i), lax.div(which, plan.n_i)
            k = jnp.where(kk == 0, 1 - c, c)
            row = i * plan.depth_h + 2 * p + k
            lanes = pl.ds(pl.multiple_of(chunk * lanes_d, lanes_d), lanes_d)
            e = [exp[row + di, :, lanes] for di in range(3)]
            sums = []
            for dj in range(3):
                total = e[0] * w_dep[dj : dj + 1, lanes]
                for di in (1, 2):
                    total = total + e[di] * w_dep[3 * di + dj : 3 * di + dj + 1, lanes]
                sums.append(total)
            summed = (
                pltpu.roll(sums[0], 1, 0)[:tile_w]
                + sums[1][:tile_w]
                + pltpu.roll(sums[2], wide - 1, 0)[:tile_w]
            )
            value = gelu(summed + b_dep[:, lanes]).astype(BF16)
            dbuf[kk, pl.ds(pl.multiple_of(i * tile_w, tile_w), tile_w), lanes] = value

        psend[p] = dot(dbuf[0], w_proj[...]).astype(BF16)
        partial_copy(p).start()
        acc[p] = dot(dbuf[1], w_proj[...])

    def forward_copy(p, q):
        s = p * plan.pw + q
        return remote(fsend.at[p, q], frecv.at[my_s], f_s.at[s], f_r.at[my_s], peer(s, c))

    def finish(p):
        partial_copy(p).wait_recv()
        own = jnp.concatenate(
            [cells[i * plan.depth_h + 2 * p + c] for i in range(plan.n_i)], axis=0
        )
        mixed = own.astype(F32) + acc[p] + precv[p].astype(F32) + b_proj[...]
        moved = dot(perm[...], mixed.astype(BF16)).astype(BF16)
        for q in range(plan.pw):
            s = p * plan.pw + q
            value = moved[q * plan.piece : (q + 1) * plan.piece]
            fsend[p, q] = value

            @pl.when(s == my_s)
            def _():
                frecv[my_s] = value

            @pl.when(s != my_s)
            def _():
                forward_copy(p, q).start()

    def step_peer(t):
        return lax.rem(mp + 1 + t, plan.ph)

    depth_rows(step_peer(0))

    @pl.loop(1, plan.ph)
    def _(t):
        depth_rows(step_peer(t))
        finish(step_peer(t - 1))

    finish(step_peer(plan.ph - 1))

    for copy in weights:
        copy.wait_recv()

    @pl.loop(0, plan.sources)
    def _(s):
        @pl.when(s != my_s)
        def _():
            remote(fsend.at[0, 0], frecv.at[s], f_s.at[s], f_r.at[s], partner).wait_recv()

    tokens = plan.sources * plan.span
    heads = half // HEAD_DIM
    lane = lax.broadcasted_iota(jnp.int32, (1, half), 1)
    head_masks = [
        ((lane >= h * HEAD_DIM) & (lane < (h + 1) * HEAD_DIM)).astype(F32) for h in range(heads)
    ]

    def return_copy(g, s, side):
        rows = pl.ds(g * plan.span, plan.span)
        return remote(
            osend.at[side, s, rows], oin.at[c, my_s, rows],
            o_s.at[side, s, g], o_r.at[c, my_s, g], peer(s, side),
        )

    for g in range(plan.groups):
        rows = slice(g * plan.span, (g + 1) * plan.span)
        mixed = frecv[:, rows, :].astype(F32).reshape(tokens, width)
        centered = mixed - jnp.mean(mixed, axis=-1, keepdims=True)
        spread = jnp.mean(centered * centered, axis=-1, keepdims=True)
        normed = (centered * lax.rsqrt(spread + 1e-05) * gain[...]).astype(BF16)
        total = mixed
        for wq, wo in ((w_qkv, w_out), (wq_other, wo_other)):
            query = dot(normed, wq[0]).astype(BF16)
            keyset = dot(normed, wq[1]).astype(BF16)
            valueset = dot(normed, wq[2]).astype(BF16)
            stacked = jnp.concatenate([query * m.astype(BF16) for m in head_masks], axis=0)
            scores = lax.dot_general(
                stacked, keyset, (((1,), (1,)), ((), ())), preferred_element_type=F32
            )
            scores = scores.reshape(heads, tokens, tokens) * HEAD_DIM ** (-0.5) + bias_s[...]
            top = jnp.max(scores, axis=-1, keepdims=True)
            weights_e = jnp.exp(scores - top)
            weights_e = weights_e / jnp.sum(weights_e, axis=-1, keepdims=True)
            mixed_v = dot(weights_e.astype(BF16).reshape(heads * tokens, tokens), valueset)
            attended = mixed_v[:tokens] * head_masks[0]
            for h in range(1, heads):
                attended = attended + mixed_v[h * tokens : (h + 1) * tokens] * head_masks[h]
            total = total + dot(attended.astype(BF16), wo[...])
        for side in range(2):
            lanes = slice(side * half, (side + 1) * half)
            value = (total[:, lanes] + bo_full[side]).astype(BF16)
            value = value.reshape(plan.sources, plan.span, half)
            osend[side, :, rows, :] = value

            @pl.when(side == c)
            def _():
                oin[c, my_s, rows] = osend[side, my_s, rows]

        @pl.loop(0, 2 * plan.sources)
        def _(t):
            s, side = lax.div(t, 2), lax.rem(t, 2)

            @pl.when(jnp.logical_not((s == my_s) & (side == c)))
            def _():
                return_copy(g, s, side).start()

    @pl.loop(0, 2 * plan.ph)
    def _(t):
        p, core = lax.div(t, 2), lax.rem(t, 2)
        for q in range(plan.pw):
            s = p * plan.pw + q

            @pl.when(jnp.logical_not((s == my_s) & (core == c)))
            def _():
                for g in range(plan.groups):
                    rows = pl.ds(g * plan.span, plan.span)
                    remote(
                        osend.at[0, 0, rows], oin.at[core, s, rows],
                        o_s.at[0, 0, g], o_r.at[core, s, g], partner,
                    ).wait_recv()
        arrived = oin[core, pl.ds(p * plan.pw, plan.pw)]
        arrived = arrived.astype(F32).reshape(plan.slab, half).astype(BF16)
        placed = dot(perm_t[...], arrived).astype(BF16)
        for i in range(plan.n_i):
            out[i * plan.depth_h + 2 * p + core] = placed[i * tile_w : (i + 1) * tile_w]

    @pl.when(has_bot)
    def _():
        down.wait_send()

    @pl.when(has_top)
    def _():
        up.wait_send()

    @pl.when(has_right)
    def _():
        rightward.wait_send()

    @pl.when(has_left)
    def _():
        leftward.wait_send()

    for copy in weights:
        copy.wait_send()

    @pl.loop(0, plan.ph)
    def _(p):
        partial_copy(p).wait_send()
        for q in range(plan.pw):
            @pl.when(p * plan.pw + q != my_s)
            def _():
                forward_copy(p, q).wait_send()

    @pl.loop(0, 2 * plan.sources)
    def _(t):
        s, side = lax.div(t, 2), lax.rem(t, 2)

        @pl.when(jnp.logical_not((s == my_s) & (side == c)))
        def _():
            for g in range(plan.groups):
                return_copy(g, s, side).wait_send()


def per_device(
    mesh_shape, cells, w_expand, b_expand, w_depth, b_depth, w_project, b_project, ln_gain,
    w_qkv, w_out, b_out,
):
    tile_h, tile_w, width = cells.shape
    plan = Plan(mesh_shape, tile_h, tile_w)
    inner = w_expand.shape[1]
    half = width // 2
    span_rows = -(-(tile_h + 2) // 16) * 16
    edge_own = np.zeros((2 * span_rows, tile_h * tile_w), np.float32)
    for r in range(tile_h):
        edge_own[1 + r, r * tile_w] = 1
        edge_own[span_rows + 1 + r, r * tile_w + tile_w - 1] = 1
    perm = plan.permutation()
    args = (
        cells, w_expand, b_expand[None], w_depth.reshape(9, inner).astype(F32), b_depth[None],
        w_project, b_project[None], ln_gain[None], w_qkv.transpose(1, 0, 2), w_out, b_out[None],
        jnp.asarray(perm, BF16), jnp.asarray(perm.T, BF16),
        jnp.asarray(plan.score_bias()), jnp.asarray(edge_own, BF16),
    )
    dma = pltpu.SemaphoreType.DMA
    vmem = pltpu.VMEM
    n = plan
    return pl.pallas_call(
        functools.partial(kernel, plan),
        out_shape=jax.ShapeDtypeStruct((tile_h, tile_w, half), BF16),
        in_specs=[pl.BlockSpec(memory_space=pltpu.VMEM)] * len(args),
        out_specs=pl.BlockSpec(memory_space=pltpu.VMEM),
        scratch_shapes=[
            vmem((tile_h + 2, tile_w + 8, inner), F32),
            vmem((2, tile_w, width), BF16),
            vmem((2, span_rows, width), BF16),
            vmem((2, span_rows, width), BF16),
            vmem((2 * span_rows, inner), F32),
            vmem((2, n.slab, inner), BF16),
            vmem((n.ph, n.slab, width), BF16),
            vmem((n.ph, n.slab, width), BF16),
            vmem((n.ph, n.slab, width), F32),
            vmem((n.ph, n.pw, n.piece, width), BF16),
            vmem((n.sources, n.piece, width), BF16),
            vmem((3, width, half), BF16),
            vmem((half, width), BF16),
            vmem((2, 1, half), F32),
            vmem((2, n.sources, n.piece, half), BF16),
            vmem((2, n.sources, n.piece, half), BF16),
            dma((2,)), dma((2,)), dma((2,)), dma((2,)), dma((3,)), dma((3,)),
            dma((n.ph,)), dma((n.ph,)), dma((n.sources,)), dma((n.sources,)),
            dma((2, n.sources, n.groups)), dma((2, n.sources, n.groups)),
        ],
        compiler_params=pltpu.CompilerParams(
            collective_id=0, has_side_effects=True, vmem_limit_bytes=60 << 20
        ),
    )(*args)


def solution(mesh):
    placed = (
        P(("grp", "gy"), "gx", None),
        P(None, "ch"),
        P("ch"),
        P(None, None, "ch"),
        P("ch"),
        P("ch", None),
        P(),
        P(),
        P(None, None, "ch"),
        P("ch", None),
        P("ch"),
    )
    return jax.shard_map(
        functools.partial(per_device, dict(mesh.shape)),
        mesh=mesh,
        in_specs=placed,
        out_specs=P(("grp", "gy"), "gx", "ch"),
        check_vma=False,
    )
```

```python
import functools

import jax
import jax.numpy as jnp
import numpy as np
from jax import lax
from jax.experimental import pallas as pl
from jax.experimental.pallas import tpu as pltpu
from jax.sharding import PartitionSpec as P

HEAD_DIM = 32
GRID = 8
MESH = pl.DeviceIdType.MESH
F32 = jnp.float32
BF16 = jnp.bfloat16


def gelu(v):
    return v * (0.5 * (1.0 + lax.erf(v * np.float32(np.sqrt(0.5)))))


def dot(a, b):
    return jnp.dot(a, b, preferred_element_type=F32)


class Plan:
    def __init__(self, mesh_shape, tile_h, tile_w):
        self.n_rows, self.n_cols = mesh_shape["gy"], mesh_shape["gx"]
        self.tile_h, self.tile_w = tile_h, tile_w
        stride_h = tile_h * self.n_rows // GRID
        stride_w = tile_w * self.n_cols // GRID
        self.depth_h, self.depth_w = min(tile_h, stride_h), min(tile_w, stride_w)
        self.steps_h, self.steps_w = stride_h // self.depth_h, stride_w // self.depth_w
        self.n_i, self.n_j = tile_h // self.depth_h, tile_w // self.depth_w
        self.ph, self.pw = GRID // self.n_i, GRID // self.n_j
        self.own_h, self.own_w = self.depth_h // self.ph, self.depth_w // self.pw
        assert self.own_h == 2
        self.n_t = self.n_i * self.n_j
        self.sources = self.ph * self.pw
        self.part_w = self.own_w // 2
        self.piece = self.part_w * self.n_t
        self.slab = self.n_i * tile_w
        groups = self.part_w
        while groups > 1 and (self.piece // groups) % 16:
            groups //= 2
        self.groups = groups
        self.span = self.piece // groups

    def permutation(self):
        out = np.zeros((self.slab, self.slab), np.float32)
        half = self.slab // 2
        for q in range(self.pw):
            for b in range(self.own_w):
                core, b_in = b // self.part_w, b % self.part_w
                for i in range(self.n_i):
                    for j in range(self.n_j):
                        row = (q * self.part_w + b_in) * self.n_t + i * self.n_j + j
                        column = j * self.depth_w + q * self.own_w + b
                        out[core * half + row, i * self.tile_w + column] = 1
        return out

    def score_bias(self):
        rows = np.arange(self.sources * self.span)
        window = (rows % self.span) // self.n_t
        return np.where(window[:, None] == window[None, :], 0.0, -1e30).astype(np.float32)


def kernel(
    plan, cells_h, w_exp_h, b_exp, w_dep_in, b_dep, w_proj_h, b_proj, gain, w_qkv_h, w_out_h,
    b_out, perm, perm_t, bias_s, edge_own, out,
    cells, w_exp, w_proj, w_qkv, w_out, w_dep,
    exp, halo, edge, colin, colexp, dbuf, dperm, psend, precv, acc, fsend, frecv,
    wq_other, wo_other, bo_full, osend, oin,
    in_s, halo_s, halo_r, col_s, col_r, w_s, w_r, p_s, p_r, f_s, f_r, o_s, o_r,
):
    tile_h, tile_w = plan.tile_h, plan.tile_w
    width = cells.shape[2]
    inner = w_exp.shape[1]
    part = plan.slab // 2
    half = width // 2
    z, x, c = lax.axis_index("gy"), lax.axis_index("gx"), lax.axis_index("ch")
    zs, xs = lax.rem(z, plan.steps_h), lax.rem(x, plan.steps_w)
    mp, mq = lax.div(z, plan.steps_h), lax.div(x, plan.steps_w)
    my_s = mp * plan.pw + mq
    last_z, last_x = plan.n_rows - 1, plan.n_cols - 1
    partner = {"ch": 1 - c}
    has_top, has_bot = z > 0, z < last_z
    has_left, has_right = x > 0, x < last_x

    def peer(s, core):
        p, q = lax.div(s, plan.pw), lax.rem(s, plan.pw)
        return {"gy": p * plan.steps_h + zs, "gx": q * plan.steps_w + xs, "ch": core}

    def remote(src, dst, send, recv, device):
        return pltpu.make_async_remote_copy(
            src_ref=src, dst_ref=dst, send_sem=send, recv_sem=recv,
            device_id=device, device_id_type=MESH,
        )

    loads = [
        pltpu.make_async_copy(src, dst, in_s.at[n])
        for n, (src, dst) in enumerate((
            (cells_h, cells), (w_exp_h, w_exp), (w_proj_h, w_proj), (w_qkv_h, w_qkv),
            (w_out_h, w_out),
        ))
    ]
    for load in loads:
        load.start()

    barrier = pltpu.get_barrier_semaphore()
    around = (
        (has_top, {"gy": jnp.maximum(z - 1, 0)}),
        (has_bot, {"gy": jnp.minimum(z + 1, last_z)}),
        (has_left, {"gx": jnp.maximum(x - 1, 0)}),
        (has_right, {"gx": jnp.minimum(x + 1, last_x)}),
    )
    count = jnp.int32(2 * plan.sources - 1)
    for there, device in around:
        @pl.when(there)
        def _():
            pl.semaphore_signal(barrier, inc=1, device_id=device, device_id_type=MESH)
        count = count + there.astype(jnp.int32)

    @pl.loop(0, 2 * plan.sources)
    def _(t):
        s, core = lax.div(t, 2), lax.rem(t, 2)

        @pl.when(jnp.logical_not((s == my_s) & (core == c)))
        def _():
            pl.semaphore_signal(barrier, inc=1, device_id=peer(s, core), device_id_type=MESH)

    down = remote(cells_h.at[tile_h - 1], halo.at[0], halo_s.at[0], halo_r.at[0], around[1][1])
    up = remote(cells_h.at[0], halo.at[1], halo_s.at[1], halo_r.at[1], around[0][1])
    rightward = remote(edge.at[1], colin.at[0], col_s.at[0], col_r.at[0], around[3][1])
    leftward = remote(edge.at[0], colin.at[1], col_s.at[1], col_r.at[1], around[2][1])
    weights = (
        remote(w_qkv_h, wq_other, w_s.at[0], w_r.at[0], partner),
        remote(w_out_h, wo_other, w_s.at[1], w_r.at[1], partner),
        remote(b_out, bo_full.at[c], w_s.at[2], w_r.at[2], partner),
    )

    for di in range(3):
        w_dep[3 * di : 3 * di + 3] = w_dep_in[di].astype(F32)
    bo_full[c] = b_out[...]
    loads[0].wait()
    loads[1].wait()

    lanes_e = 256
    rows_e = 4

    def expand(source, lanes):
        return gelu(dot(source, w_exp[:, lanes]) + b_exp[:, lanes])

    def expand_rows(first):
        source = cells[pl.ds(first, rows_e)].reshape(rows_e * tile_w, width)

        @pl.loop(0, inner // lanes_e)
        def _(t):
            lanes = pl.ds(pl.multiple_of(t * lanes_e, lanes_e), lanes_e)
            value = expand(source, lanes)
            for r in range(rows_e):
                exp[first + 1 + r, 0:tile_w, lanes] = value[r * tile_w : (r + 1) * tile_w]

    expand_rows(0)
    pl.semaphore_wait(barrier, count)

    @pl.when(has_bot)
    def _():
        down.start()

    @pl.when(has_top)
    def _():
        up.start()

    for copy in weights:
        copy.start()

    @pl.loop(1, tile_h // rows_e)
    def _(t):
        expand_rows(t * rows_e)

    for index, there, copy in ((0, has_top, down), (1, has_bot, up)):
        @pl.when(there)
        def _():
            copy.wait_recv()

        @pl.when(jnp.logical_not(there))
        def _():
            halo[index] = jnp.zeros(halo.shape[1:], BF16)

    flat = cells[...].reshape(tile_h * tile_w, width)
    span_rows = edge.shape[1]
    picked = dot(edge_own[...], flat)
    at_row = lax.broadcasted_iota(jnp.int32, (span_rows, width), 0)
    for side, col in ((0, 0), (1, tile_w - 1)):
        top = halo[0].astype(F32)[col : col + 1]
        bottom = halo[1].astype(F32)[col : col + 1]
        value = picked[side * span_rows : (side + 1) * span_rows]
        value = jnp.where(at_row == 0, top, jnp.where(at_row == tile_h + 1, bottom, value))
        edge[side] = value.astype(BF16)

    @pl.when(has_right)
    def _():
        rightward.start()

    @pl.when(has_left)
    def _():
        leftward.start()

    ok_top, ok_bot = has_top.astype(F32), has_bot.astype(F32)
    ok_left, ok_right = has_left.astype(F32), has_right.astype(F32)
    halo_flat = halo[...].reshape(2 * tile_w, width)

    @pl.loop(0, inner // lanes_e)
    def _(t):
        lanes = pl.ds(pl.multiple_of(t * lanes_e, lanes_e), lanes_e)
        value = expand(halo_flat, lanes)
        exp[0, 0:tile_w, lanes] = value[:tile_w] * ok_top
        exp[tile_h + 1, 0:tile_w, lanes] = value[tile_w:] * ok_bot

    for index, there, copy in ((0, has_left, rightward), (1, has_right, leftward)):
        @pl.when(there)
        def _():
            copy.wait_recv()

        @pl.when(jnp.logical_not(there))
        def _():
            colin[index] = jnp.zeros(colin.shape[1:], BF16)

    col_flat = colin[...].reshape(2 * span_rows, width)

    @pl.loop(0, inner // lanes_e)
    def _(t):
        lanes = pl.ds(pl.multiple_of(t * lanes_e, lanes_e), lanes_e)
        colexp[:, lanes] = expand(col_flat, lanes)

    @pl.loop(0, tile_h + 2)
    def _(r):
        row_ok = jnp.where(r == 0, ok_top, jnp.where(r == tile_h + 1, ok_bot, jnp.float32(1)))
        left = colexp[pl.ds(r, 1), :] * (row_ok * ok_left)
        right = colexp[pl.ds(span_rows + r, 1), :] * (row_ok * ok_right)
        at = lax.broadcasted_iota(jnp.int32, (8, inner), 0)
        exp[r, tile_w : tile_w + 8, :] = jnp.where(at == 0, right, left)

    lanes_d = 128
    wide = tile_w + 8

    def partial_copy(t):
        return remote(psend.at[t], precv.at[t], p_s.at[t], p_r.at[t], partner)

    def step_of(t):
        return lax.div(t, plan.ph), lax.rem(mp + 1 + lax.rem(t, plan.ph), plan.ph)

    def depth_rows(t):
        k, p = step_of(t)

        @pl.loop(0, plan.n_i * (inner // lanes_d))
        def _(u):
            chunk, i = lax.rem(u, inner // lanes_d), lax.div(u, inner // lanes_d)
            row = i * plan.depth_h + 2 * p + k
            lanes = pl.ds(pl.multiple_of(chunk * lanes_d, lanes_d), lanes_d)
            e = [exp[row + di, :, lanes] for di in range(3)]
            sums = []
            for dj in range(3):
                total = e[0] * w_dep[dj : dj + 1, lanes]
                for di in (1, 2):
                    total = total + e[di] * w_dep[3 * di + dj : 3 * di + dj + 1, lanes]
                sums.append(total)
            summed = (
                pltpu.roll(sums[0], 1, 0)[:tile_w]
                + sums[1][:tile_w]
                + pltpu.roll(sums[2], wide - 1, 0)[:tile_w]
            )
            value = gelu(summed + b_dep[:, lanes]).astype(BF16)
            dbuf[pl.ds(pl.multiple_of(i * tile_w, tile_w), tile_w), lanes] = value

        ordered = dot(perm[...], dbuf[...]).astype(BF16)
        projected = dot(ordered, w_proj[...])
        dperm[0] = projected[:part]
        dperm[1] = projected[part:]
        psend[t] = dperm[1 - c].astype(BF16)
        partial_copy(t).start()
        rows = jnp.concatenate(
            [cells[i * plan.depth_h + 2 * p + k] for i in range(plan.n_i)], axis=0
        )
        placed = dot(perm[pl.ds(pl.multiple_of(c * part, part), part)], rows)
        acc[t] = dperm[c] + placed + b_proj[...]

    def forward_copy(k, p, q):
        s = p * plan.pw + q
        return remote(
            fsend.at[k, p, q], frecv.at[k, my_s], f_s.at[k, s], f_r.at[k, my_s], peer(s, c)
        )

    def finish(t):
        k, p = step_of(t)
        partial_copy(t).wait_recv()
        mixed = (acc[t] + precv[t].astype(F32)).astype(BF16)
        for q in range(plan.pw):
            s = p * plan.pw + q
            value = mixed[q * plan.piece : (q + 1) * plan.piece]
            fsend[k, p, q] = value

            @pl.when(s == my_s)
            def _():
                frecv[k, my_s] = value

            @pl.when(s != my_s)
            def _():
                forward_copy(k, p, q).start()

    loads[2].wait()
    depth_rows(jnp.int32(0))

    @pl.loop(1, 2 * plan.ph)
    def _(t):
        depth_rows(t)
        finish(t - 1)

    finish(jnp.int32(2 * plan.ph - 1))
    loads[3].wait()
    loads[4].wait()

    for copy in weights:
        copy.wait_recv()

    def await_batch(k):
        @pl.loop(0, plan.sources)
        def _(s):
            @pl.when(s != my_s)
            def _():
                remote(
                    fsend.at[0, 0, 0], frecv.at[k, s], f_s.at[k, s], f_r.at[k, s], partner
                ).wait_recv()

    tokens = plan.sources * plan.span
    heads = half // HEAD_DIM
    lane = lax.broadcasted_iota(jnp.int32, (1, half), 1)
    head_masks = [
        ((lane >= h * HEAD_DIM) & (lane < (h + 1) * HEAD_DIM)).astype(F32) for h in range(heads)
    ]

    def return_copy(k, g, s, side):
        rows = pl.ds(g * plan.span, plan.span)
        return remote(
            osend.at[side, k, s, rows], oin.at[mp, k, c, mq, rows],
            o_s.at[side, k, s, g], o_r.at[c, k, my_s, g], peer(s, side),
        )

    for k, g in [(k, g) for k in range(2) for g in range(plan.groups)]:
        if g == 0:
            await_batch(k)
        rows = slice(g * plan.span, (g + 1) * plan.span)
        mixed = frecv[k, :, rows, :].astype(F32).reshape(tokens, width)
        centered = mixed - jnp.mean(mixed, axis=-1, keepdims=True)
        spread = jnp.mean(centered * centered, axis=-1, keepdims=True)
        normed = (centered * lax.rsqrt(spread + 1e-05) * gain[...]).astype(BF16)
        total = mixed
        for wq, wo in ((w_qkv, w_out), (wq_other, wo_other)):
            query = dot(normed, wq[0]).astype(BF16)
            keyset = dot(normed, wq[1]).astype(BF16)
            valueset = dot(normed, wq[2]).astype(BF16)
            stacked = jnp.concatenate([query * m.astype(BF16) for m in head_masks], axis=0)
            scores = lax.dot_general(
                stacked, keyset, (((1,), (1,)), ((), ())), preferred_element_type=F32
            )
            scores = scores.reshape(heads, tokens, tokens) * HEAD_DIM ** (-0.5) + bias_s[...]
            top = jnp.max(scores, axis=-1, keepdims=True)
            weights_e = jnp.exp(scores - top)
            weights_e = weights_e / jnp.sum(weights_e, axis=-1, keepdims=True)
            mixed_v = dot(weights_e.astype(BF16).reshape(heads * tokens, tokens), valueset)
            attended = mixed_v[:tokens] * head_masks[0]
            for h in range(1, heads):
                attended = attended + mixed_v[h * tokens : (h + 1) * tokens] * head_masks[h]
            total = total + dot(attended.astype(BF16), wo[...])
        for side in range(2):
            lanes = slice(side * half, (side + 1) * half)
            value = (total[:, lanes] + bo_full[side]).astype(BF16)
            value = value.reshape(plan.sources, plan.span, half)
            osend[side, k, :, rows, :] = value

            @pl.when(side == c)
            def _():
                oin[mp, k, c, mq, rows] = osend[side, k, my_s, rows]

        @pl.loop(0, 2 * plan.sources)
        def _(t):
            s, side = lax.div(t, 2), lax.rem(t, 2)

            @pl.when(jnp.logical_not((s == my_s) & (side == c)))
            def _():
                return_copy(k, g, s, side).start()

    @pl.loop(0, 2 * plan.ph)
    def _(t):
        k, p = lax.div(t, plan.ph), lax.rem(t, plan.ph)
        for q in range(plan.pw):
            s = p * plan.pw + q
            for core in range(2):
                @pl.when(jnp.logical_not((s == my_s) & (core == c)))
                def _():
                    for g in range(plan.groups):
                        rows = pl.ds(g * plan.span, plan.span)
                        remote(
                            osend.at[0, 0, 0, rows], oin.at[p, k, core, q, rows],
                            o_s.at[0, 0, 0, g], o_r.at[core, k, s, g], partner,
                        ).wait_recv()
        arrived = oin[p, k].astype(F32).reshape(plan.slab, half).astype(BF16)
        placed = dot(perm_t[...], arrived).astype(BF16)
        for i in range(plan.n_i):
            out[i * plan.depth_h + 2 * p + k] = placed[i * tile_w : (i + 1) * tile_w]

    @pl.when(has_bot)
    def _():
        down.wait_send()

    @pl.when(has_top)
    def _():
        up.wait_send()

    @pl.when(has_right)
    def _():
        rightward.wait_send()

    @pl.when(has_left)
    def _():
        leftward.wait_send()

    for copy in weights:
        copy.wait_send()

    @pl.loop(0, 2 * plan.ph)
    def _(t):
        k, p = step_of(t)
        partial_copy(t).wait_send()
        for q in range(plan.pw):
            @pl.when(p * plan.pw + q != my_s)
            def _():
                forward_copy(k, p, q).wait_send()

    @pl.loop(0, 2 * plan.sources)
    def _(t):
        s, side = lax.div(t, 2), lax.rem(t, 2)

        @pl.when(jnp.logical_not((s == my_s) & (side == c)))
        def _():
            for k in range(2):
                for g in range(plan.groups):
                    return_copy(k, g, s, side).wait_send()


def per_device(
    mesh_shape, cells, w_expand, b_expand, w_depth, b_depth, w_project, b_project, ln_gain,
    w_qkv, w_out, b_out,
):
    tile_h, tile_w, width = cells.shape
    plan = Plan(mesh_shape, tile_h, tile_w)
    inner = w_expand.shape[1]
    half = width // 2
    span_rows = -(-(tile_h + 2) // 16) * 16
    edge_own = np.zeros((2 * span_rows, tile_h * tile_w), np.float32)
    for r in range(tile_h):
        edge_own[1 + r, r * tile_w] = 1
        edge_own[span_rows + 1 + r, r * tile_w + tile_w - 1] = 1
    perm = plan.permutation()
    args = (
        cells, w_expand, b_expand[None], w_depth, b_depth[None],
        w_project, b_project[None], ln_gain[None], w_qkv.transpose(1, 0, 2), w_out, b_out[None],
        jnp.asarray(perm, BF16), jnp.asarray(perm.T, BF16),
        jnp.asarray(plan.score_bias()), jnp.asarray(edge_own, BF16),
    )
    dma = pltpu.SemaphoreType.DMA
    vmem = pltpu.VMEM
    n = plan
    return pl.pallas_call(
        functools.partial(kernel, plan),
        out_shape=jax.ShapeDtypeStruct((tile_h, tile_w, half), BF16),
        in_specs=[
            pl.BlockSpec(memory_space=pl.ANY if at in (0, 1, 5, 8, 9) else pltpu.VMEM)
            for at in range(len(args))
        ],
        out_specs=pl.BlockSpec(memory_space=pltpu.VMEM),
        scratch_shapes=[
            vmem(cells.shape, BF16), vmem(w_expand.shape, BF16), vmem(w_project.shape, BF16),
            vmem((3, width, half), BF16), vmem((half, width), BF16), vmem((9, inner), F32),
            vmem((tile_h + 2, tile_w + 8, inner), F32),
            vmem((2, tile_w, width), BF16),
            vmem((2, span_rows, width), BF16),
            vmem((2, span_rows, width), BF16),
            vmem((2 * span_rows, inner), F32),
            vmem((n.slab, inner), BF16),
            vmem((2, n.slab // 2, width), F32),
            vmem((2 * n.ph, n.slab // 2, width), BF16),
            vmem((2 * n.ph, n.slab // 2, width), BF16),
            vmem((2 * n.ph, n.slab // 2, width), F32),
            vmem((2, n.ph, n.pw, n.piece, width), BF16),
            vmem((2, n.sources, n.piece, width), BF16),
            vmem((3, width, half), BF16),
            vmem((half, width), BF16),
            vmem((2, 1, half), F32),
            vmem((2, 2, n.sources, n.piece, half), BF16),
            vmem((n.ph, 2, 2, n.pw, n.piece, half), BF16),
            dma((5,)),
            dma((2,)), dma((2,)), dma((2,)), dma((2,)), dma((3,)), dma((3,)),
            dma((2 * n.ph,)), dma((2 * n.ph,)), dma((2, n.sources)), dma((2, n.sources)),
            dma((2, 2, n.sources, n.groups)), dma((2, 2, n.sources, n.groups)),
        ],
        compiler_params=pltpu.CompilerParams(
            collective_id=0, has_side_effects=True, vmem_limit_bytes=60 << 20
        ),
    )(*args)


def solution(mesh):
    placed = (
        P(("grp", "gy"), "gx", None),
        P(None, "ch"),
        P("ch"),
        P(None, None, "ch"),
        P("ch"),
        P("ch", None),
        P(),
        P(),
        P(None, None, "ch"),
        P("ch", None),
        P("ch"),
    )
    return jax.shard_map(
        functools.partial(per_device, dict(mesh.shape)),
        mesh=mesh,
        in_specs=placed,
        out_specs=P(("grp", "gy"), "gx", "ch"),
        check_vma=False,
    )
```
